128 devices in a mesh: ctx: 64 (over x, y, z_lo, core), head: 2 (over z_hi).
Axes of the slice: x: 4, y: 4, z: 4 (z_hi: 2, z_lo: 2; z = z_hi * 2 + z_lo), core: 2. Of those that a mesh axis runs over, the one named last changes fastest.
Arguments:
- queries: bfloat16 [8, 64, 128], P('head', 'ctx'), may hold values from -192 to 192
- incoming_keys: bfloat16 [8, 8, 128], P('head'), may hold values from -6 to 6
- incoming_values: bfloat16 [8, 8, 128], P('head'), may hold values from -6 to 6
- paged_cache: bfloat16 [768, 2, 256, 1024], P('ctx', None, None, 'head'), may hold values from -6 to 6
- page_table: int32 [4, 192], replicated, may hold values from 0 to 767, as said below
- lengths: int32 [4], replicated, may hold values from 1 to 49152, as said below
Outputs:
- attended: bfloat16 [8, 64, 128], P('head', 'ctx')
The draws below stay inside these ranges and needn't reach their ends.
Inputs may be any that keep to these rules, and one draw needn't show every extreme that they name: `page_table`: a permutation of the 768 global slots: every slot holds exactly one page. `lengths`: some sequence has exactly 49152 cached tokens.
All inputs are finite; a program needn't handle non-finite values.
Results may differ from the reference program's by a relative error of at most 0.0118.
Values may be sent and summed in bfloat16 or wider, within the bound.
A program may use at most 64 MiB of HBM per device.

```python
import jax
import jax.numpy as jnp
from jax import lax

QUERY_HEADS = 64
KEY_VALUE_HEADS = 8
HEAD_SIZE = 128
PAGE_TOKENS = 256
NEW_TOKENS = 2
SEQUENCE_COUNT = 4
CACHE_SLOTS = 768
SEQUENCE_PAGES = 192


def draw_page_table(key, part):
    order = jax.random.permutation(jax.random.fold_in(key, 11), CACHE_SLOTS)
    return order.reshape(SEQUENCE_COUNT, SEQUENCE_PAGES).astype(jnp.int32)


def draw_lengths(key, part):
    most = SEQUENCE_PAGES * PAGE_TOKENS
    base_offset = jax.random.randint(jax.random.fold_in(key, 21), (SEQUENCE_COUNT,), 1, most + 1)
    chosen = jax.random.randint(jax.random.fold_in(key, 22), (), 0, SEQUENCE_COUNT)
    return jnp.where(jnp.arange(SEQUENCE_COUNT) == chosen, most, base_offset).astype(jnp.int32)


def draw_queries(key, part):
    query_rows = SEQUENCE_COUNT * NEW_TOKENS * (QUERY_HEADS // KEY_VALUE_HEADS)
    base_offset = jax.random.truncated_normal(jax.random.fold_in(key, 31), -6.0, 6.0, (KEY_VALUE_HEADS, query_rows, HEAD_SIZE), jnp.float32)
    return base_offset.astype(jnp.bfloat16)


def draw_incoming_keys(key, part):
    new_rows = SEQUENCE_COUNT * NEW_TOKENS
    base_offset = jax.random.truncated_normal(jax.random.fold_in(key, 41), -6.0, 6.0, (KEY_VALUE_HEADS, new_rows, HEAD_SIZE), jnp.float32)
    return base_offset.astype(jnp.bfloat16)


def shard_levels(rng, shape, split, smallest, high):
    factor_of, own = 1.0, jax.random.fold_in(rng, 6)
    for dim, parts in split:
        steps = jnp.exp(jax.random.uniform(jax.random.fold_in(own, dim), (parts,), jnp.float32, smallest / len(split), high / len(split)))
        factor_of = factor_of * jnp.repeat(steps, shape[dim] // parts).reshape([-1 if axis == dim else 1 for axis in range(len(shape))])
    return factor_of


def gaussian(stream_key, shape, deviation, most, pieces=(), held_as=jnp.bfloat16):
    array = jax.random.normal(stream_key, shape, jnp.float32) * deviation
    if len(pieces) > 0:
        array = shard_levels(stream_key, shape, pieces, -0.22, 0.18) * array
    return jnp.clip(array, min=-most, max=most).astype(held_as)


def setup_inputs(seed: int = 0) -> dict:
    keys = jax.random.split(jax.random.key(seed), 7)
    queries = draw_queries(jax.random.fold_in(keys[6], 71), 0)
    incoming_keys = draw_incoming_keys(jax.random.fold_in(keys[6], 71), 0)
    incoming_values = gaussian(keys[2], (KEY_VALUE_HEADS, SEQUENCE_COUNT * NEW_TOKENS, HEAD_SIZE), 1.0, 6.0, ((0, 2),))
    paged_cache = gaussian(keys[3], (CACHE_SLOTS, 2, PAGE_TOKENS, KEY_VALUE_HEADS * HEAD_SIZE), 1.0, 6.0, ((0, 64), (3, 2)))
    page_table = draw_page_table(jax.random.fold_in(keys[6], 71), 0)
    lengths = draw_lengths(jax.random.fold_in(keys[6], 71), 0)
    return dict(queries=queries, incoming_keys=incoming_keys, incoming_values=incoming_values, paged_cache=paged_cache, page_table=page_table, lengths=lengths)


NEG = -1.0e30


def reference(queries, incoming_keys, incoming_values, paged_cache, page_table, lengths):
    query_group = QUERY_HEADS // KEY_VALUE_HEADS
    scale = HEAD_SIZE ** -0.5
    causal = jnp.arange(NEW_TOKENS)[:, None] >= jnp.arange(NEW_TOKENS)[None, :]
    query_block = queries.reshape(KEY_VALUE_HEADS, SEQUENCE_COUNT, NEW_TOKENS, query_group, HEAD_SIZE)
    context_keys = incoming_keys.reshape(KEY_VALUE_HEADS, SEQUENCE_COUNT, NEW_TOKENS, HEAD_SIZE)
    context_values = incoming_values.reshape(KEY_VALUE_HEADS, SEQUENCE_COUNT, NEW_TOKENS, HEAD_SIZE)

    def one_sequence(seq):
        page_slots = jnp.take(paged_cache, page_table[seq].astype(jnp.int32), axis=0)
        page_keys = page_slots[:, 0].reshape(SEQUENCE_PAGES * PAGE_TOKENS, KEY_VALUE_HEADS, HEAD_SIZE).astype(jnp.float32)
        page_values = page_slots[:, 1].reshape(SEQUENCE_PAGES * PAGE_TOKENS, KEY_VALUE_HEADS, HEAD_SIZE).astype(jnp.float32)
        query = jnp.take(query_block, seq, axis=1).transpose(1, 0, 2, 3).astype(jnp.float32)
        fresh_keys = jnp.take(context_keys, seq, axis=1).transpose(1, 0, 2).astype(jnp.float32)
        fresh_values = jnp.take(context_values, seq, axis=1).transpose(1, 0, 2).astype(jnp.float32)
        valid = jnp.arange(SEQUENCE_PAGES * PAGE_TOKENS) < lengths[seq]
        cached = jnp.einsum("thgd,nhd->thgn", query, page_keys) * scale
        cached = jnp.where(valid, cached, NEG)
        fresh = jnp.einsum("thgd,uhd->thgu", query, fresh_keys) * scale
        fresh_mask = causal[:, None, None, :]
        fresh = jnp.where(fresh_mask, fresh, NEG)
        top = jnp.maximum(jnp.max(cached, axis=-1), jnp.max(fresh, axis=-1))
        cached_w = jnp.where(valid, jnp.exp(cached - top[..., None]), 0.0)
        fresh_w = jnp.where(fresh_mask, jnp.exp(fresh - top[..., None]), 0.0)
        total = jnp.sum(cached_w, axis=-1) + jnp.sum(fresh_w, axis=-1)
        cached_r = cached_w.astype(jnp.bfloat16).astype(jnp.float32)
        fresh_r = fresh_w.astype(jnp.bfloat16).astype(jnp.float32)
        mixed = jnp.einsum("thgn,nhd->thgd", cached_r, page_values) + jnp.einsum("thgu,uhd->thgd", fresh_r, fresh_values)
        return (mixed / total[..., None]).transpose(1, 0, 2, 3).astype(jnp.bfloat16)

    stacked_rows = lax.map(one_sequence, jnp.arange(SEQUENCE_COUNT))
    return stacked_rows.transpose(1, 0, 2, 3, 4).reshape(KEY_VALUE_HEADS, SEQUENCE_COUNT * NEW_TOKENS * query_group, HEAD_SIZE)
```

```python
import functools

import jax
import jax.numpy as jnp
from jax import lax
from jax.experimental import pallas as pl
from jax.experimental.pallas import tpu as pltpu
from jax.sharding import PartitionSpec as P

QUERY_HEADS = 64
KEY_VALUE_HEADS = 8
HEAD_SIZE = 128
NEW_TOKENS = 2

LOG2E = 1.4426950408889634
MASKED = -1e30
FLOOR = -1e29
CODE = 512
SHARED = (((1,), (1,)), ((), ()))


def first_max(values):
    return functools.reduce(jnp.maximum, values)


def kernel(
    n,
    table_hbm,
    lengths_hbm,
    queries_hbm,
    keys_hbm,
    values_hbm,
    cache_hbm,
    out_ref,
    cache,
    table,
    lengths,
    own_query,
    fresh_keys,
    fresh_values,
    query,
    gathered,
    partial,
    received,
    local_sem,
    cache_sem,
    query_sems,
    partial_sems,
):
    me = lax.axis_index("ctx")
    slots, _, page, width = cache.shape
    kv_local = width // HEAD_SIZE
    seq_count, seq_pages = table.shape
    seq_rows = n // seq_count
    group = seq_rows // NEW_TOKENS
    factor = HEAD_SIZE ** (-0.5) * LOG2E

    small = [
        pltpu.make_async_copy(source, target, local_sem.at[i])
        for i, (source, target) in enumerate(
            (
                (queries_hbm, own_query),
                (table_hbm, table),
                (lengths_hbm, lengths),
                (keys_hbm, fresh_keys),
                (values_hbm, fresh_values),
            )
        )
    ]
    for copy in small:
        copy.start()
    pages = [
        pltpu.make_async_copy(cache_hbm.at[k], cache.at[k], cache_sem.at[k])
        for k in range(slots)
    ]
    for copy in pages:
        copy.start()

    barrier = pltpu.get_barrier_semaphore()

    def greet(j, carry):
        pl.semaphore_signal(barrier, inc=1, device_id={"ctx": lax.rem(me + j, n)})
        return carry

    lax.fori_loop(1, n, greet, 0)

    small[0].wait()
    for h in range(kv_local):
        query[pl.ds(h, 1), :] = own_query[h].astype(jnp.float32)
        gathered[me, pl.ds(h, 1), :] = own_query[h].astype(jnp.float32)
    pl.semaphore_wait(barrier, n - 1)

    def send_query(j, carry):
        pltpu.make_async_remote_copy(
            src_ref=query,
            dst_ref=gathered.at[me],
            send_sem=query_sems.at[0],
            recv_sem=query_sems.at[1],
            device_id={"ctx": lax.rem(me + j, n)},
        ).start()
        return carry

    lax.fori_loop(1, n, send_query, 0)

    for copy in small[1:]:
        copy.wait()

    of_seq = lax.broadcasted_iota(jnp.int32, (seq_count, seq_pages), 0)
    of_page = lax.broadcasted_iota(jnp.int32, (seq_count, seq_pages), 1)
    length = jnp.zeros((seq_count, seq_pages), jnp.int32)
    for s in range(seq_count):
        length = jnp.where(of_seq == s, lengths[s], length)
    held = jnp.clip(length - of_page * page, 0, page)
    code = (of_seq * CODE + held).astype(jnp.float32)
    entries = table[...]
    codes = [
        jnp.sum(
            jnp.where(entries == me * slots + k, code, 0.0), axis=(0, 1), keepdims=True
        )
        for k in range(slots)
    ]
    slot_seq = []
    slot_held = []
    for k in range(slots):
        seq = functools.reduce(
            jnp.add,
            [(codes[k] >= float(CODE * s)).astype(jnp.float32) for s in range(1, seq_count)],
        )
        slot_seq.append(seq)
        slot_held.append((codes[k] - float(CODE) * seq).astype(jnp.int32))

    row_seq = me // seq_rows
    row_step = lax.rem(me, seq_rows) // group
    token = lax.broadcasted_iota(jnp.int32, (seq_count * NEW_TOKENS, 1), 0)
    visible = (token // NEW_TOKENS == row_seq) & (lax.rem(token, NEW_TOKENS) <= row_step)
    fresh = []
    for h in range(kv_local):
        q = own_query[h].astype(jnp.float32)
        score = jnp.sum(q * fresh_keys[h].astype(jnp.float32), axis=1, keepdims=True)
        score = jnp.where(visible, score, MASKED)
        top = jnp.max(score, axis=0, keepdims=True)
        weight = jnp.where(visible, jnp.exp2((score - top) * factor), 0.0)
        total = jnp.sum(weight, axis=0, keepdims=True)
        rounded = weight.astype(jnp.bfloat16).astype(jnp.float32)
        mixed = jnp.sum(
            rounded * fresh_values[h].astype(jnp.float32), axis=0, keepdims=True
        )
        fresh.append((top * factor, total, mixed))

    for copy in pages:
        copy.wait()
    pltpu.make_async_copy(
        gathered.at[pl.ds(0, n - 1)], gathered.at[pl.ds(0, n - 1)], query_sems.at[1]
    ).wait()

    by_head = [gathered[:, h, :] for h in range(kv_local)]
    position = lax.broadcasted_iota(jnp.int32, (1, page), 1)
    blank = jnp.zeros((seq_rows, HEAD_SIZE), jnp.float32)
    tops, totals, mixes = [], [], []
    for k in range(slots):
        chosen = []
        for h in range(kv_local):
            rows = by_head[h][:seq_rows]
            for s in range(1, seq_count):
                rows = jnp.where(
                    slot_seq[k] == float(s),
                    by_head[h][s * seq_rows : (s + 1) * seq_rows],
                    rows,
                )
            chosen.append(rows)
        scores = []
        for h in range(0, kv_local, 2):
            left = jnp.concatenate(
                [
                    jnp.concatenate([chosen[h], blank], axis=1),
                    jnp.concatenate([blank, chosen[h + 1]], axis=1),
                ],
                axis=0,
            ).astype(jnp.bfloat16)
            keys = cache[k, 0, :, h * HEAD_SIZE : (h + 2) * HEAD_SIZE]
            scores.append(
                lax.dot_general(left, keys, SHARED, preferred_element_type=jnp.float32)
            )
        score = jnp.concatenate(scores, axis=0)
        score = jnp.where(position < slot_held[k], score, MASKED)
        top = jnp.maximum(jnp.max(score, axis=1, keepdims=True), FLOOR)
        weight = jnp.exp2((score - top) * factor)
        tops.append(top)
        totals.append(jnp.sum(weight, axis=1, keepdims=True))
        rounded = weight.astype(jnp.bfloat16)
        mixed = []
        for h in range(0, kv_local, 2):
            values = cache[k, 1, :, h * HEAD_SIZE : (h + 2) * HEAD_SIZE]
            both = jnp.dot(
                rounded[h * seq_rows : (h + 2) * seq_rows],
                values,
                preferred_element_type=jnp.float32,
            )
            mixed.append(both[:seq_rows, :HEAD_SIZE])
            mixed.append(both[seq_rows:, HEAD_SIZE:])
        mixes.append(jnp.concatenate(mixed, axis=0))

    for s in range(seq_count):
        inside = [slot_seq[k] == float(s) for k in range(slots)]
        top = first_max([jnp.where(inside[k], tops[k], FLOOR) for k in range(slots)])
        total = jnp.zeros_like(totals[0])
        mixed = jnp.zeros_like(mixes[0])
        for k in range(slots):
            share = jnp.where(inside[k], jnp.exp2((tops[k] - top) * factor), 0.0)
            total = total + share * totals[k]
            mixed = mixed + share * mixes[k]
        some = total > 0.0
        safe = jnp.where(some, total, 1.0)
        mixed = mixed / safe
        mass = jnp.where(some, top * factor + jnp.log2(safe), MASKED)
        mass = jnp.broadcast_to(mass, mixed.shape)
        rows = pl.ds(s * seq_rows, seq_rows)
        for h in range(kv_local):
            part = slice(h * seq_rows, (h + 1) * seq_rows)
            partial[rows, h, :] = mixed[part]
            partial[rows, kv_local + h, :] = mass[part]

    def send_partial(j, carry):
        peer = lax.rem(me + j, n)
        pltpu.make_async_remote_copy(
            src_ref=partial.at[peer],
            dst_ref=received.at[me],
            send_sem=partial_sems.at[0],
            recv_sem=partial_sems.at[1],
            device_id={"ctx": peer},
        ).start()
        return carry

    lax.fori_loop(1, n, send_partial, 0)
    received[me] = partial[me]

    pltpu.make_async_copy(
        received.at[pl.ds(0, n - 1)], received.at[pl.ds(0, n - 1)], partial_sems.at[1]
    ).wait()
    for h in range(kv_local):
        fresh_top, fresh_total, fresh_mixed = fresh[h]
        mixed = received[:, h, :]
        mass = received[:, kv_local + h, :]
        top = jnp.maximum(jnp.max(mass, axis=0, keepdims=True), fresh_top)
        share = jnp.exp2(mass - top)
        fresh_share = jnp.exp2(fresh_top - top)
        total = jnp.sum(share, axis=0, keepdims=True) + fresh_share * fresh_total
        sum_ = jnp.sum(share * mixed, axis=0, keepdims=True) + fresh_share * fresh_mixed
        out_ref[h] = (sum_ / total).astype(jnp.bfloat16)

    pltpu.make_async_copy(
        gathered.at[pl.ds(0, n - 1)], gathered.at[pl.ds(0, n - 1)], query_sems.at[0]
    ).wait()
    pltpu.make_async_copy(
        received.at[pl.ds(0, n - 1)], received.at[pl.ds(0, n - 1)], partial_sems.at[0]
    ).wait()


def solution(mesh):
    n = mesh.shape["ctx"]

    def on_device(queries, incoming_keys, incoming_values, paged_cache, page_table, lengths):
        kv_local = queries.shape[0]
        anywhere = pl.BlockSpec(memory_space=pl.ANY)
        return pl.pallas_call(
            functools.partial(kernel, n),
            out_shape=jax.ShapeDtypeStruct(queries.shape, queries.dtype),
            in_specs=[anywhere] * 6,
            out_specs=pl.BlockSpec(memory_space=pltpu.VMEM),
            scratch_shapes=[
                pltpu.VMEM(paged_cache.shape, paged_cache.dtype),
                pltpu.VMEM(page_table.shape, page_table.dtype),
                pltpu.SMEM(lengths.shape, lengths.dtype),
                pltpu.VMEM(queries.shape, queries.dtype),
                pltpu.VMEM(incoming_keys.shape, incoming_keys.dtype),
                pltpu.VMEM(incoming_values.shape, incoming_values.dtype),
                pltpu.VMEM((kv_local, HEAD_SIZE), jnp.float32),
                pltpu.VMEM((n, kv_local, HEAD_SIZE), jnp.float32),
                pltpu.VMEM((n, 2 * kv_local, HEAD_SIZE), jnp.float32),
                pltpu.VMEM((n, 2 * kv_local, HEAD_SIZE), jnp.float32),
                pltpu.SemaphoreType.DMA((5,)),
                pltpu.SemaphoreType.DMA((paged_cache.shape[0],)),
                pltpu.SemaphoreType.DMA((2,)),
                pltpu.SemaphoreType.DMA((2,)),
            ],
            compiler_params=pltpu.CompilerParams(collective_id=0, has_side_effects=True),
        )(page_table, lengths, queries, incoming_keys, incoming_values, paged_cache)

    in_specs = (
        P("head", "ctx", None),
        P("head", None, None),
        P("head", None, None),
        P("ctx", None, None, "head"),
        P(),
        P(),
    )
    return jax.shard_map(
        on_device,
        mesh=mesh,
        in_specs=in_specs,
        out_specs=P("head", "ctx", None),
        check_vma=False,
    )
```

```python
import functools

import jax
import jax.numpy as jnp
from jax import lax
from jax.experimental import pallas as pl
from jax.experimental.pallas import tpu as pltpu
from jax.sharding import PartitionSpec as P

QUERY_HEADS = 64
KEY_VALUE_HEADS = 8
HEAD_SIZE = 128
NEW_TOKENS = 2

LOG2E = 1.4426950408889634
MASKED = -1e30
FLOOR = -1e29
CODE = 512
SUBLANES = 8
SHARED = (((1,), (1,)), ((), ()))


def kernel(
    n,
    table_hbm,
    lengths_hbm,
    queries_hbm,
    keys_hbm,
    values_hbm,
    cache_hbm,
    out_ref,
    cache,
    table,
    lengths,
    own_query,
    fresh_keys,
    fresh_values,
    query,
    gathered,
    marks,
    bias,
    wide,
    partial,
    received,
    local_sem,
    cache_sem,
    query_sems,
    partial_sems,
):
    me = lax.axis_index("ctx")
    slots, _, page, width = cache.shape
    kv_local = width // HEAD_SIZE
    seq_count, seq_pages = table.shape
    seq_rows = n // seq_count
    group = seq_rows // NEW_TOKENS
    factor = HEAD_SIZE ** (-0.5) * LOG2E
    tiles = kv_local * seq_rows // SUBLANES

    my_seq = me // seq_rows
    my_place = lax.rem(me, seq_rows)
    seq_at = [lax.rem(my_seq + d, seq_count) for d in range(seq_count)]
    place_at = [lax.rem(my_place + d, seq_rows) for d in range(seq_rows)]
    seq_order = sorted(range(seq_count), key=lambda d: -min(d, seq_count - d))
    place_order = sorted(range(seq_rows), key=lambda d: -min(d, seq_rows - d))
    others = [(d, e) for d in seq_order for e in place_order if d or e]

    def peer(d, e):
        return seq_at[d] * seq_rows + place_at[e]

    small = [
        pltpu.make_async_copy(source, target, local_sem.at[i])
        for i, (source, target) in enumerate(
            (
                (queries_hbm, own_query),
                (table_hbm, table),
                (lengths_hbm, lengths),
                (keys_hbm, fresh_keys),
                (values_hbm, fresh_values),
            )
        )
    ]
    small[0].start()
    barrier = pltpu.get_barrier_semaphore()
    for d, e in others:
        pl.semaphore_signal(barrier, inc=1, device_id={"ctx": peer(d, e)})
    for copy in small[1:]:
        copy.start()
    pages = [
        pltpu.make_async_copy(cache_hbm.at[k], cache.at[k], cache_sem.at[k])
        for k in range(slots)
    ]
    for copy in pages:
        copy.start()

    small[0].wait()
    for h in range(kv_local):
        row = own_query[pl.ds(h, 1), :].astype(jnp.float32)
        query[pl.ds(h, 1), :] = row
        gathered[me, pl.ds(h, 1), :] = row
    pl.semaphore_wait(barrier, n - 1)

    for d, e in others:
        pltpu.make_async_remote_copy(
            src_ref=query,
            dst_ref=gathered.at[me],
            send_sem=query_sems.at[0],
            recv_sem=query_sems.at[1],
            device_id={"ctx": peer(d, e)},
        ).start()

    for copy in small[1:]:
        copy.wait()

    of_seq = lax.broadcasted_iota(jnp.int32, (seq_count, seq_pages), 0)
    of_page = lax.broadcasted_iota(jnp.int32, (seq_count, seq_pages), 1)
    length = jnp.zeros((seq_count, seq_pages), jnp.int32)
    for s in range(seq_count):
        length = jnp.where(of_seq == s, lengths[s], length)
    held = jnp.clip(length - of_page * page, 0, page)
    code = (of_seq * CODE + held).astype(jnp.float32)
    entries = table[...]
    position = lax.broadcasted_iota(jnp.int32, (SUBLANES, page), 1).astype(jnp.float32)
    for k in range(slots):
        found = jnp.where(entries == me * slots + k, code, 0.0)
        found = jnp.sum(found, axis=(0, 1), keepdims=True)
        found = jnp.broadcast_to(found, (SUBLANES, HEAD_SIZE))
        count = found
        for s in range(seq_count):
            inside = (found >= float(CODE * s)) & (found < float(CODE * (s + 1)))
            marks[k, s] = jnp.where(inside, 1.0, 0.0)
            count = jnp.where(inside, found - float(CODE * s), count)
        count = jnp.concatenate([count] * (page // HEAD_SIZE), axis=1)
        bias[k] = jnp.where(position < count, 0.0, MASKED)

    row_step = my_place // group
    token = lax.broadcasted_iota(jnp.int32, (seq_count * NEW_TOKENS, 1), 0)
    visible = (token // NEW_TOKENS == my_seq) & (lax.rem(token, NEW_TOKENS) <= row_step)
    fresh = []
    for h in range(kv_local):
        q = own_query[pl.ds(h, 1), :].astype(jnp.float32)
        score = jnp.sum(q * fresh_keys[h].astype(jnp.float32), axis=1, keepdims=True)
        score = jnp.where(visible, score, MASKED)
        top = jnp.max(score, axis=0, keepdims=True)
        weight = jnp.where(visible, jnp.exp2((score - top) * factor), 0.0)
        total = jnp.sum(weight, axis=0, keepdims=True)
        rounded = weight.astype(jnp.bfloat16).astype(jnp.float32)
        mixed = jnp.sum(
            rounded * fresh_values[h].astype(jnp.float32), axis=0, keepdims=True
        )
        fresh.append((top * factor, total, mixed))

    for copy in pages:
        copy.wait()
    arrived = gathered.at[pl.ds(0, n - 1)]
    pltpu.make_async_copy(arrived, arrived, query_sems.at[1]).wait()

    by_head = [
        gathered[:, h, :].reshape(n // SUBLANES, SUBLANES, HEAD_SIZE) for h in range(kv_local)
    ]
    seq_tiles = seq_rows // SUBLANES
    blank = jnp.zeros((seq_rows, HEAD_SIZE), jnp.float32)

    def pick(k, choices):
        chosen = choices[0]
        for s in range(1, seq_count):
            chosen = jnp.where(marks[k, s][None] > 0.5, choices[s], chosen)
        return chosen

    scores = []
    tops = [jnp.full((tiles, SUBLANES, HEAD_SIZE), FLOOR, jnp.float32)] * seq_count
    for k in range(slots):
        chosen = [
            pick(
                k, [by_head[h][s * seq_tiles : (s + 1) * seq_tiles] for s in range(seq_count)]
            ).reshape(seq_rows, HEAD_SIZE)
            for h in range(kv_local)
        ]
        score = []
        for h in range(0, kv_local, 2):
            left = jnp.concatenate(
                [
                    jnp.concatenate([chosen[h], blank], axis=1),
                    jnp.concatenate([blank, chosen[h + 1]], axis=1),
                ],
                axis=0,
            ).astype(jnp.bfloat16)
            keys = cache[k, 0, :, h * HEAD_SIZE : (h + 2) * HEAD_SIZE]
            score.append(
                lax.dot_general(left, keys, SHARED, preferred_element_type=jnp.float32)
            )
        score = jnp.concatenate(score, axis=0).reshape(tiles, SUBLANES, page)
        score = score + bias[k][None]
        scores.append(score)
        top = functools.reduce(
            jnp.maximum,
            [score[:, :, i : i + HEAD_SIZE] for i in range(0, page, HEAD_SIZE)],
        )
        for s in range(seq_count):
            tops[s] = jnp.maximum(
                tops[s], jnp.where(marks[k, s][None] > 0.5, top, FLOOR)
            )
    tops = [
        jnp.broadcast_to(jnp.max(top, axis=2, keepdims=True), top.shape) for top in tops
    ]

    sums, mixes = [], []
    for k in range(slots):
        top = pick(k, tops)
        top = jnp.concatenate([top] * (page // HEAD_SIZE), axis=2)
        weight = jnp.exp2((scores[k] - top) * factor)
        sums.append(
            functools.reduce(
                jnp.add,
                [weight[:, :, i : i + HEAD_SIZE] for i in range(0, page, HEAD_SIZE)],
            )
        )
        rounded = weight.reshape(kv_local * seq_rows, page).astype(jnp.bfloat16)
        mixed = []
        for h in range(0, kv_local, 2):
            values = cache[k, 1, :, h * HEAD_SIZE : (h + 2) * HEAD_SIZE]
            both = jnp.dot(
                rounded[h * seq_rows : (h + 2) * seq_rows],
                values,
                preferred_element_type=jnp.float32,
            )
            mixed.append(both[:seq_rows, :HEAD_SIZE])
            mixed.append(both[seq_rows:, HEAD_SIZE:])
        mixes.append(
            jnp.concatenate(mixed, axis=0).reshape(tiles, SUBLANES, HEAD_SIZE)
        )

    lane = lax.broadcasted_iota(jnp.int32, (1, 1, HEAD_SIZE), 2)
    for s in range(seq_count):
        total = jnp.zeros_like(sums[0])
        mixed = jnp.zeros_like(mixes[0])
        for k in range(slots):
            mark = marks[k, s][None]
            total = total + mark * sums[k]
            mixed = mixed + mark * mixes[k]
        total = jnp.sum(total, axis=2, keepdims=True)
        some = total > 0.0
        safe = jnp.where(some, total, 1.0)
        mixed = mixed / safe
        mass = jnp.where(some, tops[s] * factor + jnp.log2(safe), MASKED)
        high = mass.astype(jnp.bfloat16).astype(jnp.float32)
        rest = mass - high
        middle = rest.astype(jnp.bfloat16).astype(jnp.float32)
        low = rest - middle
        mass = jnp.where(
            lane == 0, high, jnp.where(lane == 1, middle, jnp.where(lane == 2, low, 0.0))
        )
        mixed = mixed.reshape(kv_local * seq_rows, HEAD_SIZE)
        mass = mass.reshape(kv_local * seq_rows, HEAD_SIZE)
        rows = pl.ds(s * seq_rows, seq_rows)
        for h in range(kv_local):
            part = slice(h * seq_rows, (h + 1) * seq_rows)
            wide[rows, h, :] = mixed[part]
            wide[rows, kv_local + h, :] = mass[part]
        partial[rows] = wide[rows].astype(jnp.bfloat16)

    for d, e in others:
        partner = peer(d, e)
        pltpu.make_async_remote_copy(
            src_ref=partial.at[partner],
            dst_ref=received.at[me],
            send_sem=partial_sems.at[0],
            recv_sem=partial_sems.at[1],
            device_id={"ctx": partner},
        ).start()
    received[me] = partial[me]

    arrived = received.at[pl.ds(0, n - 1)]
    pltpu.make_async_copy(arrived, arrived, partial_sems.at[1]).wait()
    wide[...] = received[...].astype(jnp.float32)
    for h in range(kv_local):
        fresh_top, fresh_total, fresh_mixed = fresh[h]
        mixed = wide[:, h, :]
        mass = jnp.sum(wide[:, kv_local + h, :], axis=1, keepdims=True)
        top = jnp.maximum(jnp.max(mass, axis=0, keepdims=True), fresh_top)
        share = jnp.exp2(mass - top)
        fresh_share = jnp.exp2(fresh_top - top)
        total = jnp.sum(share, axis=0, keepdims=True) + fresh_share * fresh_total
        whole = jnp.sum(share * mixed, axis=0, keepdims=True) + fresh_share * fresh_mixed
        out_ref[pl.ds(h, 1), :] = (whole / total).astype(jnp.bfloat16)

    sent = gathered.at[pl.ds(0, n - 1)]
    pltpu.make_async_copy(sent, sent, query_sems.at[0]).wait()
    sent = received.at[pl.ds(0, n - 1)]
    pltpu.make_async_copy(sent, sent, partial_sems.at[0]).wait()


def solution(mesh):
    n = mesh.shape["ctx"]

    def on_device(queries, incoming_keys, incoming_values, paged_cache, page_table, lengths):
        kv_local = queries.shape[0]
        slots, _, page, _ = paged_cache.shape
        row = queries.reshape(kv_local, HEAD_SIZE)
        anywhere = pl.BlockSpec(memory_space=pl.ANY)
        attended = pl.pallas_call(
            functools.partial(kernel, n),
            out_shape=jax.ShapeDtypeStruct(row.shape, row.dtype),
            in_specs=[anywhere] * 6,
            out_specs=pl.BlockSpec(memory_space=pltpu.VMEM),
            scratch_shapes=[
                pltpu.VMEM(paged_cache.shape, paged_cache.dtype),
                pltpu.VMEM(page_table.shape, page_table.dtype),
                pltpu.SMEM(lengths.shape, lengths.dtype),
                pltpu.VMEM(row.shape, row.dtype),
                pltpu.VMEM(incoming_keys.shape, incoming_keys.dtype),
                pltpu.VMEM(incoming_values.shape, incoming_values.dtype),
                pltpu.VMEM((kv_local, HEAD_SIZE), jnp.float32),
                pltpu.VMEM((n, kv_local, HEAD_SIZE), jnp.float32),
                pltpu.VMEM((slots, page_table.shape[0], SUBLANES, HEAD_SIZE), jnp.float32),
                pltpu.VMEM((slots, SUBLANES, page), jnp.float32),
                pltpu.VMEM((n, 2 * kv_local, HEAD_SIZE), jnp.float32),
                pltpu.VMEM((n, 2 * kv_local, HEAD_SIZE), jnp.bfloat16),
                pltpu.VMEM((n, 2 * kv_local, HEAD_SIZE), jnp.bfloat16),
                pltpu.SemaphoreType.DMA((5,)),
                pltpu.SemaphoreType.DMA((slots,)),
                pltpu.SemaphoreType.DMA((2,)),
                pltpu.SemaphoreType.DMA((2,)),
            ],
            compiler_params=pltpu.CompilerParams(collective_id=0, has_side_effects=True),
        )(page_table, lengths, row, incoming_keys, incoming_values, paged_cache)
        return attended.reshape(queries.shape)

    in_specs = (
        P("head", "ctx", None),
        P("head", None, None),
        P("head", None, None),
        P("ctx", None, None, "head"),
        P(),
        P(),
    )
    return jax.shard_map(
        on_device,
        mesh=mesh,
        in_specs=in_specs,
        out_specs=P("head", "ctx", None),
        check_vma=False,
    )
```

```python
import functools

import jax
import jax.numpy as jnp
from jax import lax
from jax.experimental import pallas as pl
from jax.experimental.pallas import tpu as pltpu
from jax.sharding import PartitionSpec as P

QUERY_HEADS = 64
KEY_VALUE_HEADS = 8
HEAD_SIZE = 128
NEW_TOKENS = 2

LOG2E = 1.4426950408889634
MASKED = -1e30
FLOOR = -1e29
CODE = 512
SUBLANES = 8
SHARED = (((1,), (1,)), ((), ()))


def kernel(
    n,
    table_hbm,
    lengths_hbm,
    queries_hbm,
    keys_hbm,
    values_hbm,
    cache_hbm,
    out_ref,
    cache,
    table,
    lengths,
    own_query,
    fresh_keys,
    fresh_values,
    query,
    gathered,
    marks,
    bias,
    wide,
    partial,
    received,
    local_sem,
    cache_sem,
    query_sems,
    partial_sems,
):
    me = lax.axis_index("ctx")
    slots, _, page, width = cache.shape
    kv_local = width // HEAD_SIZE
    seq_count, seq_pages = table.shape
    seq_rows = n // seq_count
    group = seq_rows // NEW_TOKENS
    factor = HEAD_SIZE ** (-0.5) * LOG2E
    tiles = kv_local * seq_rows // SUBLANES

    my_seq = me // seq_rows
    my_place = lax.rem(me, seq_rows)
    seq_at = [lax.rem(my_seq + d, seq_count) for d in range(seq_count)]
    place_at = [lax.rem(my_place + d, seq_rows) for d in range(seq_rows)]
    seq_order = sorted(range(seq_count), key=lambda d: -min(d, seq_count - d))
    place_order = sorted(range(seq_rows), key=lambda d: -min(d, seq_rows - d))
    others = [(d, e) for d in seq_order for e in place_order if d or e]

    def peer(d, e):
        return seq_at[d] * seq_rows + place_at[e]

    small = [
        pltpu.make_async_copy(source, target, local_sem.at[i])
        for i, (source, target) in enumerate(
            (
                (queries_hbm, own_query),
                (table_hbm, table),
                (lengths_hbm, lengths),
                (keys_hbm, fresh_keys),
                (values_hbm, fresh_values),
            )
        )
    ]
    small[0].start()
    barrier = pltpu.get_barrier_semaphore()
    for d, e in others:
        pl.semaphore_signal(barrier, inc=1, device_id={"ctx": peer(d, e)})
    for copy in small[1:]:
        copy.start()
    pages = [
        pltpu.make_async_copy(cache_hbm.at[k], cache.at[k], cache_sem.at[k])
        for k in range(slots)
    ]
    for copy in pages:
        copy.start()

    small[0].wait()
    for h in range(kv_local):
        row = own_query[pl.ds(h, 1), :].astype(jnp.float32)
        query[pl.ds(h, 1), :] = row
        gathered[me, pl.ds(h, 1), :] = row
    pl.semaphore_wait(barrier, n - 1)

    for d, e in others:
        pltpu.make_async_remote_copy(
            src_ref=query,
            dst_ref=gathered.at[me],
            send_sem=query_sems.at[0],
            recv_sem=query_sems.at[1],
            device_id={"ctx": peer(d, e)},
        ).start()

    for copy in small[1:]:
        copy.wait()

    of_seq = lax.broadcasted_iota(jnp.int32, (seq_count, seq_pages), 0)
    of_page = lax.broadcasted_iota(jnp.int32, (seq_count, seq_pages), 1)
    length = jnp.zeros((seq_count, seq_pages), jnp.int32)
    for s in range(seq_count):
        length = jnp.where(of_seq == s, lengths[s], length)
    held = jnp.clip(length - of_page * page, 0, page)
    code = (of_seq * CODE + held).astype(jnp.float32)
    entries = table[...]
    position = lax.broadcasted_iota(jnp.int32, (SUBLANES, page), 1).astype(jnp.float32)
    for k in range(slots):
        found = jnp.where(entries == me * slots + k, code, 0.0)
        found = jnp.sum(found, axis=(0, 1), keepdims=True)
        found = jnp.broadcast_to(found, (SUBLANES, HEAD_SIZE))
        count = found
        for s in range(seq_count):
            inside = (found >= float(CODE * s)) & (found < float(CODE * (s + 1)))
            marks[k, s] = jnp.where(inside, 1.0, 0.0)
            count = jnp.where(inside, found - float(CODE * s), count)
        count = jnp.concatenate([count] * (page // HEAD_SIZE), axis=1)
        bias[k] = jnp.where(position < count, 0.0, MASKED)

    row_step = my_place // group
    token = lax.broadcasted_iota(jnp.int32, (seq_count * NEW_TOKENS, 1), 0)
    visible = (token // NEW_TOKENS == my_seq) & (lax.rem(token, NEW_TOKENS) <= row_step)
    fresh = []
    for h in range(kv_local):
        q = own_query[pl.ds(h, 1), :].astype(jnp.float32)
        score = jnp.sum(q * fresh_keys[h].astype(jnp.float32), axis=1, keepdims=True)
        score = jnp.where(visible, score, MASKED)
        top = jnp.max(score, axis=0, keepdims=True)
        weight = jnp.where(visible, jnp.exp2((score - top) * factor), 0.0)
        total = jnp.sum(weight, axis=0, keepdims=True)
        rounded = weight.astype(jnp.bfloat16).astype(jnp.float32)
        mixed = jnp.sum(
            rounded * fresh_values[h].astype(jnp.float32), axis=0, keepdims=True
        )
        fresh.append((top * factor, total, mixed))

    for copy in pages:
        copy.wait()
    arrived = gathered.at[pl.ds(0, n - 1)]
    pltpu.make_async_copy(arrived, arrived, query_sems.at[1]).wait()

    by_head = [
        gathered[:, h, :].reshape(n // SUBLANES, SUBLANES, HEAD_SIZE) for h in range(kv_local)
    ]
    seq_tiles = seq_rows // SUBLANES
    blank = jnp.zeros((seq_rows, HEAD_SIZE), jnp.float32)

    def pick(k, choices):
        chosen = choices[0]
        for s in range(1, seq_count):
            chosen = jnp.where(marks[k, s][None] > 0.5, choices[s], chosen)
        return chosen

    scores = []
    tops = [jnp.full((tiles, SUBLANES, HEAD_SIZE), FLOOR, jnp.float32)] * seq_count
    for k in range(slots):
        chosen = [
            pick(
                k, [by_head[h][s * seq_tiles : (s + 1) * seq_tiles] for s in range(seq_count)]
            ).reshape(seq_rows, HEAD_SIZE)
            for h in range(kv_local)
        ]
        score = []
        for h in range(0, kv_local, 2):
            left = jnp.concatenate(
                [
                    jnp.concatenate([chosen[h], blank], axis=1),
                    jnp.concatenate([blank, chosen[h + 1]], axis=1),
                ],
                axis=0,
            ).astype(jnp.bfloat16)
            keys = cache[k, 0, :, h * HEAD_SIZE : (h + 2) * HEAD_SIZE]
            score.append(
                lax.dot_general(left, keys, SHARED, preferred_element_type=jnp.float32)
            )
        score = jnp.concatenate(score, axis=0).reshape(tiles, SUBLANES, page)
        score = score + bias[k][None]
        scores.append(score)
        top = functools.reduce(
            jnp.maximum,
            [score[:, :, i : i + HEAD_SIZE] for i in range(0, page, HEAD_SIZE)],
        )
        for s in range(seq_count):
            tops[s] = jnp.maximum(
                tops[s], jnp.where(marks[k, s][None] > 0.5, top, FLOOR)
            )
    tops = [
        jnp.broadcast_to(jnp.max(top, axis=2, keepdims=True), top.shape) for top in tops
    ]

    sums, mixes = [], []
    for k in range(slots):
        top = pick(k, tops)
        top = jnp.concatenate([top] * (page // HEAD_SIZE), axis=2)
        weight = jnp.exp2((scores[k] - top) * factor)
        sums.append(
            functools.reduce(
                jnp.add,
                [weight[:, :, i : i + HEAD_SIZE] for i in range(0, page, HEAD_SIZE)],
            )
        )
        rounded = weight.reshape(kv_local * seq_rows, page).astype(jnp.bfloat16)
        mixed = []
        for h in range(0, kv_local, 2):
            values = cache[k, 1, :, h * HEAD_SIZE : (h + 2) * HEAD_SIZE]
            both = jnp.dot(
                rounded[h * seq_rows : (h + 2) * seq_rows],
                values,
                preferred_element_type=jnp.float32,
            )
            mixed.append(both[:seq_rows, :HEAD_SIZE])
            mixed.append(both[seq_rows:, HEAD_SIZE:])
        mixes.append(
            jnp.concatenate(mixed, axis=0).reshape(tiles, SUBLANES, HEAD_SIZE)
        )

    lane = lax.broadcasted_iota(jnp.int32, (1, 1, HEAD_SIZE), 2)
    for s in range(seq_count):
        total = jnp.zeros_like(sums[0])
        mixed = jnp.zeros_like(mixes[0])
        for k in range(slots):
            mark = marks[k, s][None]
            total = total + mark * sums[k]
            mixed = mixed + mark * mixes[k]
        total = jnp.sum(total, axis=2, keepdims=True)
        some = total > 0.0
        safe = jnp.where(some, total, 1.0)
        mixed = mixed / safe
        mass = jnp.where(some, tops[s] * factor + jnp.log2(safe), MASKED)
        high = mass.astype(jnp.bfloat16).astype(jnp.float32)
        rest = mass - high
        middle = rest.astype(jnp.bfloat16).astype(jnp.float32)
        low = rest - middle
        mass = jnp.where(
            lane == 0, high, jnp.where(lane == 1, middle, jnp.where(lane == 2, low, 0.0))
        )
        mixed = mixed.reshape(kv_local * seq_rows, HEAD_SIZE)
        mass = mass.reshape(kv_local * seq_rows, HEAD_SIZE)
        rows = pl.ds(s * seq_rows, seq_rows)
        for h in range(kv_local):
            part = slice(h * seq_rows, (h + 1) * seq_rows)
            wide[rows, h, :] = mixed[part]
            wide[rows, kv_local + h, :] = mass[part]
        partial[rows] = wide[rows].astype(jnp.bfloat16)

    for d, e in others:
        partner = peer(d, e)
        pltpu.make_async_remote_copy(
            src_ref=partial.at[partner],
            dst_ref=received.at[me],
            send_sem=partial_sems.at[0],
            recv_sem=partial_sems.at[1],
            device_id={"ctx": partner},
        ).start()
    received[me] = partial[me]

    arrived = received.at[pl.ds(0, n - 1)]
    pltpu.make_async_copy(arrived, arrived, partial_sems.at[1]).wait()
    wide[...] = received[...].astype(jnp.float32)
    for h in range(kv_local):
        fresh_top, fresh_total, fresh_mixed = fresh[h]
        mixed = wide[:, h, :]
        mass = jnp.sum(wide[:, kv_local + h, :], axis=1, keepdims=True)
        top = jnp.maximum(jnp.max(mass, axis=0, keepdims=True), fresh_top)
        share = jnp.exp2(mass - top)
        fresh_share = jnp.exp2(fresh_top - top)
        total = jnp.sum(share, axis=0, keepdims=True) + fresh_share * fresh_total
        whole = jnp.sum(share * mixed, axis=0, keepdims=True) + fresh_share * fresh_mixed
        out_ref[pl.ds(h, 1), :] = (whole / total).astype(jnp.bfloat16)

    sent = gathered.at[pl.ds(0, n - 1)]
    pltpu.make_async_copy(sent, sent, query_sems.at[0]).wait()
    sent = received.at[pl.ds(0, n - 1)]
    pltpu.make_async_copy(sent, sent, partial_sems.at[0]).wait()


def solution(mesh):
    n = mesh.shape["ctx"]

    def on_device(queries, incoming_keys, incoming_values, paged_cache, page_table, lengths):
        kv_local = queries.shape[0]
        slots, _, page, _ = paged_cache.shape
        row = queries.reshape(kv_local, HEAD_SIZE)
        anywhere = pl.BlockSpec(memory_space=pl.ANY)
        attended = pl.pallas_call(
            functools.partial(kernel, n),
            out_shape=pltpu.VMEM(row.shape, row.dtype),
            in_specs=[anywhere] * 6,
            out_specs=pl.BlockSpec(memory_space=pltpu.VMEM),
            scratch_shapes=[
                pltpu.VMEM(paged_cache.shape, paged_cache.dtype),
                pltpu.VMEM(page_table.shape, page_table.dtype),
                pltpu.SMEM(lengths.shape, lengths.dtype),
                pltpu.VMEM(row.shape, row.dtype),
                pltpu.VMEM(incoming_keys.shape, incoming_keys.dtype),
                pltpu.VMEM(incoming_values.shape, incoming_values.dtype),
                pltpu.VMEM((kv_local, HEAD_SIZE), jnp.float32),
                pltpu.VMEM((n, kv_local, HEAD_SIZE), jnp.float32),
                pltpu.VMEM((slots, page_table.shape[0], SUBLANES, HEAD_SIZE), jnp.float32),
                pltpu.VMEM((slots, SUBLANES, page), jnp.float32),
                pltpu.VMEM((n, 2 * kv_local, HEAD_SIZE), jnp.float32),
                pltpu.VMEM((n, 2 * kv_local, HEAD_SIZE), jnp.bfloat16),
                pltpu.VMEM((n, 2 * kv_local, HEAD_SIZE), jnp.bfloat16),
                pltpu.SemaphoreType.DMA((5,)),
                pltpu.SemaphoreType.DMA((slots,)),
                pltpu.SemaphoreType.DMA((2,)),
                pltpu.SemaphoreType.DMA((2,)),
            ],
            compiler_params=pltpu.CompilerParams(collective_id=0, has_side_effects=True),
        )(page_table, lengths, row, incoming_keys, incoming_values, paged_cache)
        return attended.reshape(queries.shape)

    in_specs = (
        P("head", "ctx", None),
        P("head", None, None),
        P("head", None, None),
        P("ctx", None, None, "head"),
        P(),
        P(),
    )
    return jax.shard_map(
        on_device,
        mesh=mesh,
        in_specs=in_specs,
        out_specs=P("head", "ctx", None),
        check_vma=False,
    )
```
